512 devices in a mesh: rows: 32 (over x, y, core), upd: 16 (over z).
Axes of the slice: x: 4, y: 4, z: 16, core: 2. Of those that a mesh axis runs over, the one named last changes fastest.
Arguments:
- tile_factors: bfloat16 [32, 128, 1024, 128], P('rows', 'upd'), may hold values from -6 to 6
- panel_factors: bfloat16 [128, 1024, 128], P('upd', 'rows'), may hold values from -0.1875 to 0.1875
- nonnull: int32 [32, 128], P('rows', 'upd'), may hold values from 0 to 1, as said below
- sketch: float32 [64, 1024], replicated, may hold values from -6 to 6
Outputs:
- update_factors: float32 [32, 1024, 128], P('rows', 'upd')
The draws below stay inside these ranges and needn't reach their ends.
Inputs may be any that keep to these rules, and one draw needn't show every extreme that they name: In every aligned block of 8 update indices the first one is nonnull for every tile row.
All inputs are finite; a program needn't handle non-finite values.
Results may differ from the reference program's by a relative error of at most 0.0003.
Values may be sent and summed in bfloat16 or wider, within the bound.
No kernel may reach another device: no remote copies, remote signals or barrier semaphores. Data moves between devices by JAX's collectives and lax.ppermute only.
A program may use at most 64 MiB of HBM per device.

```python
import jax
import jax.numpy as jnp
from jax import lax

B = 1024
R = 64
KD = 8
K = 128
TILES = 32
N_UPD = 16


def draw_nonnull(key, part):
    bits = jax.random.randint(key, (TILES, K), 0, 2).astype(jnp.int32)
    first = jnp.arange(K) % KD == 0
    return jnp.where(first[None, :], 1, bits).astype(jnp.int32)


def block_scale(key, extent, cuts, low, top_value):
    def one(axis_at, parts):
        steps = jax.random.uniform(jax.random.fold_in(jax.random.fold_in(key, 6), axis_at), (parts,), jnp.float32, low / len(cuts), top_value / len(cuts))
        return jnp.repeat(jnp.exp(steps), extent[axis_at] // parts).reshape((-1,) + (1,) * (len(extent) - axis_at - 1))

    factor_of = one(*cuts[0])
    for cut in cuts[1:]:
        factor_of = factor_of * one(*cut)
    return factor_of


def gaussian(key, dims, spread, reach, pieces=(), kind=jnp.bfloat16):
    array = jax.random.normal(key, dims, jnp.float32) * spread
    if len(pieces) > 0:
        array = block_scale(key, dims, pieces, -0.22, 0.18) * array
    return jnp.clip(array, min=-reach, max=reach).astype(kind)


def setup_inputs(seed: int = 0) -> dict:
    streams_of = jax.random.split(jax.random.key(seed), 5)
    return {
        "tile_factors": gaussian(streams_of[0], (TILES, K, B, 2 * R), 1.0, 6.0, ((0, 32), (1, 16))),
        "panel_factors": gaussian(streams_of[1], (K, B, 2 * R), B ** -0.5, 0.1875, ((0, 16), (1, 32))),
        "nonnull": draw_nonnull(jax.random.fold_in(streams_of[4], 71), 0),
        "sketch": gaussian(streams_of[3], (R, B), 1.0, 6.0, (), jnp.float32),
    }


def compress(lefts, rights, sketch):
    hi = lax.Precision.HIGHEST
    proj = jnp.einsum('nbr,sb->nrs', rights, sketch, precision=hi)
    span = jnp.einsum('nbr,nrs->bs', lefts, proj, precision=hi)
    gram = jnp.dot(span.T, span, precision=hi)
    order = gram.shape[0]
    shift = 0.001 * jnp.trace(gram) / order + 1e-20
    gram = gram + shift * jnp.eye(order, dtype=gram.dtype)
    chol = jnp.linalg.cholesky(gram)
    basis = lax.linalg.triangular_solve(chol, span, left_side=False, lower=True, transpose_a=True)
    coef = jnp.einsum('nbr,bs->nrs', lefts, basis, precision=hi)
    image = jnp.einsum('nbr,nrs->bs', rights, coef, precision=hi)
    return (basis, image)

def one_row(tiles, mask, panel, sketch):
    rank = tiles.shape[2] // 2
    own_left = tiles[:, :, :rank].astype(jnp.float32)
    own_right = tiles[:, :, rank:].astype(jnp.float32)
    inner = jnp.einsum('kbr,kbs->krs', own_right, panel[:, :, rank:].astype(jnp.float32))
    lefts = jnp.einsum('kbr,krs->kbs', own_left, inner, precision=lax.Precision.HIGHEST)
    lefts = lefts * mask.astype(jnp.float32)[:, None, None]
    rights = panel[:, :, :rank].astype(jnp.float32)
    lefts = lefts.reshape(N_UPD, KD, B, rank)
    rights = rights.reshape(N_UPD, KD, B, rank)
    basis, image = jax.vmap(lambda a, b: compress(a, b, sketch))(lefts, rights)
    nodes = jnp.concatenate([basis, image], axis=-1)
    count = N_UPD
    while count > 1:
        pairs = nodes.reshape(count // 2, 2, B, 2 * rank)
        basis, image = jax.vmap(lambda p: compress(p[:, :, :rank], p[:, :, rank:], sketch))(pairs)
        nodes = jnp.concatenate([basis, image], axis=-1)
        count = count // 2
    scale = jnp.float32(B) ** 0.5
    return jnp.concatenate([nodes[0, :, :rank] * scale, nodes[0, :, rank:] / scale], axis=-1)

def reference(tile_factors, panel_factors, nonnull, sketch):
    return lax.map(lambda item: one_row(item[0], item[1], panel_factors, sketch), (tile_factors, nonnull))
```

```python
import jax
import jax.numpy as jnp
from jax import lax
from jax.experimental import pallas as pl
from jax.experimental.pallas import tpu as pltpu
from jax.sharding import PartitionSpec as P


F32 = jnp.float32
BF16 = jnp.bfloat16
R = 64
NN = (((1,), (0,)), ((), ()))
NT = (((1,), (1,)), ((), ()))
TN = (((0,), (0,)), ((), ()))
VMEM = pl.BlockSpec(memory_space=pltpu.VMEM)
SMEM = pl.BlockSpec(memory_space=pltpu.SMEM)


def mm(a, b, dims=NN):
    return lax.dot_general(a, b, dims, preferred_element_type=F32)


def split(x):
    hi = x.astype(BF16)
    return hi, (x - hi.astype(F32)).astype(BF16)


def dot3(a, b, dims=NN):
    ah, al = split(a)
    bh, bl = split(b)
    return mm(ah, bh, dims) + (mm(ah, bl, dims) + mm(al, bh, dims))


def eye_mask():
    r = lax.broadcasted_iota(jnp.int32, (R, R), 0)
    c = lax.broadcasted_iota(jnp.int32, (R, R), 1)
    return r == c


def shift_of(gram, diag):
    t = jnp.sum(jnp.where(diag, gram, 0.0), axis=1, keepdims=True)
    t = jnp.sum(t, axis=0, keepdims=True)
    return (0.001 / R) * t + 1e-20


def eliminate(mats, chol=False):
    n, wide = R // 8, (8, 2 * R)
    eye = jnp.where(eye_mask(), 1.0, 0.0).astype(F32)
    blocks = []
    for m in mats:
        aug = jnp.concatenate([eye, m], axis=1)
        blocks.append([aug[8 * i : 8 * i + 8, :] for i in range(n)])
    sub = lax.broadcasted_iota(jnp.int32, wide, 0)
    done = [[None] * n for _ in mats]

    def splat(v):
        return jnp.broadcast_to(v, wide)

    for j in range(0, R, 4):
        jb, js = j // 8, j % 8
        for blk, out in zip(blocks, done):
            r0, r1, r2, r3 = [splat(blk[jb][js + a : js + a + 1, :]) for a in range(4)]

            def at(row, b):
                return splat(row[:, R + j + b : R + j + b + 1])

            p00, p01, p02, p03 = [at(r0, b) for b in range(4)]
            p11, p12, p13 = [at(r1, b) for b in range(1, 4)]
            p22, p23, p33 = at(r2, 2), at(r2, 3), at(r3, 3)
            i1 = 1.0 / (p00 * p11 - p01 * p01)
            a00, a01, a11 = p11 * i1, -p01 * i1, p00 * i1
            t00, t01 = a00 * p02 + a01 * p12, a00 * p03 + a01 * p13
            t10, t11 = a01 * p02 + a11 * p12, a01 * p03 + a11 * p13
            s22 = p22 - (p02 * t00 + p12 * t10)
            s23 = p23 - (p02 * t01 + p12 * t11)
            s33 = p33 - (p03 * t01 + p13 * t11)
            i2 = 1.0 / (s22 * s33 - s23 * s23)
            z2 = r2 - (t00 * r0 + t10 * r1)
            z3 = r3 - (t01 * r0 + t11 * r1)
            q2 = (s33 * i2) * z2 - (s23 * i2) * z3
            q3 = (s22 * i2) * z3 - (s23 * i2) * z2
            q0 = (a00 * r0 + a01 * r1) - (t00 * q2 + t01 * q3)
            q1 = (a01 * r0 + a11 * r1) - (t10 * q2 + t11 * q3)
            for i in range(jb, n):
                if i == jb and js == 4:
                    continue
                c = [splat(blk[i][:, R + j + t : R + j + t + 1]) for t in range(4)]
                up = (c[0] * q0 + c[1] * q1) + (c[2] * q2 + c[3] * q3)
                blk[i] = blk[i] - (jnp.where(sub >= 4, up, 0.0) if i == jb else up)
            if chol:
                g0 = lax.rsqrt(p00)
                l1 = p01 * g0
                w0 = r0 * g0
                g1 = lax.rsqrt(p11 - l1 * l1)
                w1 = (r1 - l1 * w0) * g1
                ratio = s23 / s22
                w2 = z2 * lax.rsqrt(s22)
                w3 = (z3 - ratio * z2) * lax.rsqrt(s33 - s23 * ratio)
                keep = (w0, w1, w2, w3)
            else:
                keep = (q0, q1, q2, q3)
            acc = out[jb] if js else jnp.zeros(wide, F32)
            for t in range(4):
                acc = jnp.where(sub == js + t, keep[t], acc)
            out[jb] = acc
    res = []
    for blk, out in zip(blocks, done):
        rows = jnp.concatenate(out, axis=0)[:, :R]
        res.append(rows if chol else dot3(jnp.concatenate(blk, axis=0)[:, :R], rows, TN))
    return res


def inverses(grams):
    diag = eye_mask()
    shifts = [shift_of(g, diag) for g in grams]
    mats = [jnp.where(diag, g * (1.0 / s) + 1.0, g * (1.0 / s)) for g, s in zip(grams, shifts)]
    return shifts, eliminate(mats)


def ident():
    return jnp.where(eye_mask(), 1.0, 0.0).astype(F32)


def place():
    core, z = lax.axis_index("rows") % 2, lax.axis_index("upd")
    g = z // 4
    o = 2 - (g + core) % 2
    return core, z, g, o, 2 * o - 3


def interleave(core, own_ref, oth_ref, pan):
    for c in range(16):
        pan[:, c, pl.ds(core, 1), :, :] = own_ref[c][:, None]
        pan[:, c, pl.ds(1 - core, 1), :, :] = oth_ref[c][:, None]


def leaf_y(w_ref, tile_ref, own_ref, oth_ref, sk_ref, y_ref, inner_ref, pan):
    core = place()[0]
    interleave(core, own_ref, oth_ref, pan)
    sh, sl = split(sk_ref[...])
    r = lax.broadcasted_iota(jnp.int32, (R, 2 * R), 0)
    c = lax.broadcasted_iota(jnp.int32, (R, 2 * R), 1)
    pick = jnp.where(c == r + R, 1.0, 0.0).astype(BF16)
    zero = jnp.zeros((R, R), F32)
    acc = jnp.zeros((R, 1024), F32)
    for k in range(8):
        tile = tile_ref[k]
        pan_k = pan[k].reshape(1024, 2 * R)
        vt = mm(pick, tile, NT).astype(BF16)
        res = mm(jnp.concatenate([sh, sl, vt], axis=0), pan_k)
        proj = (res[:R] + res[R : 2 * R])[:, :R]
        inner = res[2 * R :][:, R:] * w_ref[k].astype(F32)
        inner_ref[k] = inner
        dt = jnp.concatenate([dot3(proj, inner, NT), zero], axis=1)
        dh, dl = split(dt)
        out = mm(jnp.concatenate([dh, dl], axis=0), tile, NT)
        acc = acc + (out[:R] + out[R:])
    y_ref[...] = acc


def leaf_x(tile_ref, own_ref, oth_ref, y_ref, inner_ref, x_ref, pan):
    core = place()[0]
    interleave(core, own_ref, oth_ref, pan)
    yh, yl = split(y_ref[...])
    ys = jnp.concatenate([yh, yl], axis=0)
    zero = jnp.zeros((R, R), F32)
    acc = jnp.zeros((R, 1024), F32)
    for k in range(8):
        pan_k = pan[k].reshape(1024, 2 * R)
        ht = mm(ys, tile_ref[k])
        ht = (ht[:R] + ht[R:])[:, :R]
        et = jnp.concatenate([dot3(ht, inner_ref[k]), zero], axis=1)
        eh, el = split(et)
        out = mm(jnp.concatenate([eh, el], axis=0), pan_k, NT)
        acc = acc + (out[:R] + out[R:])
    x_ref[...] = acc


def lanes(mats):
    return jnp.concatenate(mats, axis=1)


def rows_of(mats):
    return jnp.concatenate(mats, axis=0)


def put_shift(s):
    return jnp.broadcast_to(s, (8, 2 * R))


def group_y(y0, y1, y2, y3, out_ref, k_ref, j_ref, s_ref):
    stack = rows_of([y0[...], y1[...], y2[...], y3[...]])
    ah, al = split(stack)
    gram = mm(ah, ah, NT) + (mm(ah, al, NT) + mm(al, ah, NT))
    k_ref[...] = gram
    eye = ident()
    shifts, js = inverses([gram[R * u : R * u + R, R * u : R * u + R] for u in range(4)])
    rs = [eye - j for j in js]
    pair_r = [lanes(rs[0:2]), lanes(rs[2:4])]
    grams = []
    for m in range(2):
        kp = gram[2 * R * m : 2 * R * m + 2 * R, 2 * R * m : 2 * R * m + 2 * R]
        grams.append(dot3(dot3(pair_r[m], kp), rows_of(rs[2 * m : 2 * m + 2])))
    shifts2, js2 = inverses(grams)
    pt = lanes([dot3(eye - js2[m], pair_r[m]) for m in range(2)])
    ph, plo = split(pt)
    out_ref[...] = mm(ph, ah) + (mm(ph, al) + mm(plo, ah))
    for u, j in enumerate(js + js2):
        j_ref[u] = j
    for u, s in enumerate(shifts + shifts2):
        s_ref[u] = put_shift(1.0 / s)


def group_x(x0, x1, x2, x3, k_ref, j_ref, s_ref, send_ref, keep_ref):
    eye = ident()
    gram = k_ref[...]
    js = [j_ref[u] for u in range(6)]
    ss = [s_ref[u][:1, :1] for u in range(6)]
    rs = [eye - j for j in js]
    pt, q1 = [], []
    for m in range(2):
        pr = lanes(rs[2 * m : 2 * m + 2])
        kp = gram[2 * R * m : 2 * R * m + 2 * R, 2 * R * m : 2 * R * m + 2 * R]
        rk = dot3(pr, kp)
        q1.append(
            lanes([dot3(rk[:, :R] * ss[2 * m], js[2 * m]), dot3(rk[:, R:] * ss[2 * m + 1], js[2 * m + 1])])
        )
        pt.append(dot3(rs[4 + m], pr))
    pk = dot3(lanes(pt), gram)
    qt = []
    for m in range(2):
        t = dot3(pk[:, 2 * R * m : 2 * R * m + 2 * R], rows_of(rs[2 * m : 2 * m + 2]))
        t = dot3(t * ss[4 + m], js[4 + m])
        qt.append(dot3(t, q1[m]))
    qh, ql = split(lanes(qt))
    refs = (x0, x1, x2, x3)
    g = place()[2]
    sib = g + 1 - 2 * (g % 2)
    for dst, blocks in ((send_ref, (sib, 3 - sib)), (keep_ref, (g, 3 - g))):
        for i, block in enumerate(blocks):
            at = pl.multiple_of(block * 256, 256)
            xh, xl = split(rows_of([x[:, pl.ds(at, 256)] for x in refs]))
            dst[:, 256 * i : 256 * i + 256] = mm(qh, xh) + (mm(qh, xl) + mm(ql, xh))


def merge_y(y0, y1, out_ref, k_ref, j_ref, s_ref):
    ah, al = split(rows_of([y0[...], y1[...]]))
    gram = mm(ah, ah, NT) + (mm(ah, al, NT) + mm(al, ah, NT))
    k_ref[...] = gram
    eye = ident()
    shifts, js = inverses([gram[R * u : R * u + R, R * u : R * u + R] for u in range(2)])
    ph, plo = split(lanes([eye - j for j in js]))
    out_ref[...] = mm(ph, ah) + (mm(ph, al) + mm(plo, ah))
    for u in range(2):
        j_ref[u] = js[u]
        s_ref[u] = put_shift(1.0 / shifts[u])


def merge_q(gram, js, ss):
    eye = ident()
    rk = dot3(lanes([eye - j for j in js]), gram)
    return lanes([dot3(rk[:, R * u : R * u + R] * ss[u], js[u]) for u in range(2)])


def merge_x(x0, x1, k_ref, j_ref, s_ref, send_ref, keep_ref):
    qt = merge_q(k_ref[...], [j_ref[u] for u in range(2)], [s_ref[u][:1, :1] for u in range(2)])
    out = dot3(qt, rows_of([x0[...], x1[...]]))
    keep_ref[...] = out[:, :256]
    send_ref[...] = out[:, 256:]


def root_y(y0, y1, w_ref, f_ref):
    ah, al = split(rows_of([y0[...], y1[...]]))
    gram = mm(ah, ah, NT) + (mm(ah, al, NT) + mm(al, ah, NT))
    eye = ident()
    shifts, js = inverses([gram[R * u : R * u + R, R * u : R * u + R] for u in range(2)])
    rs = [eye - j for j in js]
    pr = lanes(rs)
    g = dot3(dot3(pr, gram), rows_of(rs))
    diag = eye_mask()
    s = shift_of(g, diag)
    rec = 1.0 / s
    (ci,) = eliminate([jnp.where(diag, g * rec + 1.0, g * rec)], chol=True)
    ci = ci * lax.rsqrt(s)
    f_ref[...] = dot3(ci, merge_q(gram, js, [1.0 / v for v in shifts]))
    at = pl.multiple_of(place()[2] * 256, 256)
    yr = rows_of([y0[:, pl.ds(at, 256)], y1[:, pl.ds(at, 256)]])
    w_ref[...] = dot3(dot3(ci, pr), yr) * 32.0


def root_out(w_ref, f_ref, x0, x1, o0, o1, o2, o3, buf):
    zt = dot3(f_ref[...], rows_of([x0[...], x1[...]])) * (1.0 / 32.0)
    buf[...] = rows_of([w_ref[...], zt]).T
    _, z, g, o, e = place()
    mine = jnp.where(z == 4 * g + o, 1, 0)

    def block(j):
        return buf[pl.ds(pl.multiple_of(j * R, R), R), :]

    o0[...] = jnp.where(jnp.full((R, 2 * R), mine) == 1, block(o), 0.0)
    o1[...], o2[...], o3[...] = block(o + e), block(o - e), block(o - 2 * e)


def shape(*dims, dtype=F32):
    return jax.ShapeDtypeStruct(dims, dtype)


def call(fn, outs, n_smem, args, scratch=(), flops=10**8):
    specs = [SMEM] * n_smem + [VMEM] * (len(args) - n_smem)
    many = isinstance(outs, (tuple, list))
    kernel = pl.pallas_call(
        fn,
        out_shape=outs,
        in_specs=specs,
        out_specs=[VMEM] * len(outs) if many else VMEM,
        scratch_shapes=list(scratch),
        cost_estimate=pl.CostEstimate(flops=flops, bytes_accessed=10**6, transcendentals=0),
        compiler_params=pltpu.CompilerParams(vmem_limit_bytes=20 * 2**20),
    )
    return kernel(*args)


OWNERS = ((2, 5, 10, 13), (1, 6, 9, 14))
SIDE = ((1, -1, 1, -1), (-1, 1, -1, 1))


def over_rows(per_core, rows, upd):
    return [(r * upd + a, r * upd + b) for r in range(rows) for a, b in per_core[r % 2]]


def tables(rows, upd):
    member = []
    for off in (1, -1, -2):
        member.append([[(o + off * e, o) for o, e in zip(OWNERS[c], SIDE[c])] for c in range(2)])
    third = [[(OWNERS[c][i], OWNERS[c][i ^ 1]) for i in range(4)] for c in range(2)]
    fourth = [[(OWNERS[c][i], OWNERS[c][3 - i]) for i in range(4)] for c in range(2)]
    back = [[[(b, a) for a, b in m[c]] for c in range(2)] for m in member]
    full = lambda p: over_rows(p, rows, upd)
    return [full(m) for m in member], full(third), full(fourth), [full(m) for m in back]


def tree(y, leaf_x_of, rows, upd):
    members, third, fourth, back = tables(rows, upd)

    def send(v, perm):
        return lax.ppermute(v, ("rows", "upd"), perm)

    ys = [y] + [send(y, m) for m in members]
    x = leaf_x_of(y)
    xs = [x] + [send(x, m) for m in members]
    sizes = (shape(R, 1024), shape(256, 256), shape(6, R, R), shape(6, 8, 128))
    y2, k2, j2, s2 = call(group_y, sizes, 0, ys)
    y2h = send(y2, third)
    xsend, xkeep = call(group_x, (shape(R, 512), shape(R, 512)), 0, [*xs, k2, j2, s2])
    xh = send(xsend, third)
    sizes = (shape(R, 1024), shape(128, 128), shape(2, R, R), shape(2, 8, 128))
    y3, k3, j3, s3 = call(merge_y, sizes, 0, [y2, y2h])
    y3h = send(y3, fourth)
    xsend, xkeep = call(merge_x, (shape(R, 256), shape(R, 256)), 0, [xkeep, xh, k3, j3, s3])
    xh = send(xsend, fourth)
    wt, f = call(root_y, (shape(R, 256), shape(R, 128)), 0, [y3, y3h])
    buf = [pltpu.VMEM((256, 128), F32)]
    outs = call(root_out, [shape(R, 128)] * 4, 0, [wt, f, xkeep, xh], scratch=buf)
    res = outs[0]
    for o, p in zip(outs[1:], back):
        res = res + send(o, p)
    return res


def local_update(tiles, own, oth, nonnull, sketch, rows, upd):
    pan = pltpu.VMEM((8, 16, 2, 32, 128), BF16)
    tiles = tiles.reshape(8, 1024, 2 * R)
    y, inner = call(
        leaf_y, (shape(R, 1024), shape(8, R, R)), 1, [nonnull, tiles, own, oth, sketch], scratch=[pan]
    )

    def leaf_x_of(y):
        return call(leaf_x, shape(R, 1024), 0, [tiles, own, oth, y, inner], scratch=[pan])

    return tree(y, leaf_x_of, rows, upd)


def body(tile_factors, panel_factors, nonnull, sketch):
    rows, upd = lax.axis_size("rows"), lax.axis_size("upd")
    same = [[2 * i + c for i in range(rows // 2)] for c in range(2)]
    blocks = jnp.broadcast_to(panel_factors[None], (rows // 2,) + panel_factors.shape)
    own = lax.all_to_all(blocks, "rows", 0, 0, axis_index_groups=same)
    oth = lax.ppermute(own, "rows", [(i, i ^ 1) for i in range(rows)])
    return local_update(tile_factors[0], own, oth, nonnull[0], sketch, rows, upd)[None]


def solution(mesh):
    in_specs = (P("rows", "upd", None, None), P("upd", "rows", None), P("rows", "upd"), P())
    out_specs = P("rows", "upd", None)
    return jax.shard_map(body, mesh=mesh, in_specs=in_specs, out_specs=out_specs, check_vma=False)
```

```python
import jax
import jax.numpy as jnp
from jax import lax
from jax.experimental import pallas as pl
from jax.experimental.pallas import tpu as pltpu
from jax.sharding import PartitionSpec as P


F32 = jnp.float32
BF16 = jnp.bfloat16
R = 64
NN = (((1,), (0,)), ((), ()))
NT = (((1,), (1,)), ((), ()))
TN = (((0,), (0,)), ((), ()))
VMEM = pl.BlockSpec(memory_space=pltpu.VMEM)
SMEM = pl.BlockSpec(memory_space=pltpu.SMEM)


def mm(a, b, dims=NN):
    return lax.dot_general(a, b, dims, preferred_element_type=F32)


def split(x):
    hi = x.astype(BF16)
    return hi, (x - hi.astype(F32)).astype(BF16)


def dot3(a, b, dims=NN):
    ah, al = split(a)
    bh, bl = split(b)
    return mm(ah, bh, dims) + (mm(ah, bl, dims) + mm(al, bh, dims))


def eye_mask():
    r = lax.broadcasted_iota(jnp.int32, (R, R), 0)
    c = lax.broadcasted_iota(jnp.int32, (R, R), 1)
    return r == c


def shift_of(gram, diag):
    t = jnp.sum(jnp.where(diag, gram, 0.0), axis=1, keepdims=True)
    t = jnp.sum(t, axis=0, keepdims=True)
    return (0.001 / R) * t + 1e-20


def eliminate(mats, chol=False):
    n, wide = R // 8, (8, 2 * R)
    eye = jnp.where(eye_mask(), 1.0, 0.0).astype(F32)
    blocks = []
    for m in mats:
        aug = jnp.concatenate([eye, m], axis=1)
        blocks.append([aug[8 * i : 8 * i + 8, :] for i in range(n)])
    sub = lax.broadcasted_iota(jnp.int32, wide, 0)
    zero = jnp.minimum(jnp.abs(blocks[0][0]), 0.0)
    done = [[None] * n for _ in mats]

    def splat(v):
        return jnp.broadcast_to(v, wide)

    for j in range(0, R, 4):
        jb, js = j // 8, j % 8
        for blk, out in zip(blocks, done):
            r0, r1, r2, r3 = [splat(blk[jb][js + a : js + a + 1, :]) for a in range(4)]
            near = [splat(blk[jb][:, R + j + t : R + j + t + 1]) + zero for t in range(4)]

            def at(a, b):
                return splat(near[b][js + a : js + a + 1, :])

            p00, p01, p02, p03 = [at(0, b) for b in range(4)]
            p11, p12, p13 = [at(1, b) for b in range(1, 4)]
            p22, p23, p33 = at(2, 2), at(2, 3), at(3, 3)
            i1 = 1.0 / (p00 * p11 - p01 * p01)
            a00, a01, a11 = p11 * i1, -p01 * i1, p00 * i1
            t00, t01 = a00 * p02 + a01 * p12, a00 * p03 + a01 * p13
            t10, t11 = a01 * p02 + a11 * p12, a01 * p03 + a11 * p13
            s22 = p22 - (p02 * t00 + p12 * t10)
            s23 = p23 - (p02 * t01 + p12 * t11)
            s33 = p33 - (p03 * t01 + p13 * t11)
            i2 = 1.0 / (s22 * s33 - s23 * s23)
            z2 = r2 - (t00 * r0 + t10 * r1)
            z3 = r3 - (t01 * r0 + t11 * r1)
            q2 = (s33 * i2) * z2 - (s23 * i2) * z3
            q3 = (s22 * i2) * z3 - (s23 * i2) * z2
            q0 = (a00 * r0 + a01 * r1) - (t00 * q2 + t01 * q3)
            q1 = (a01 * r0 + a11 * r1) - (t10 * q2 + t11 * q3)
            for i in range(jb, n):
                if i == jb and js == 4:
                    continue
                c = near if i == jb else [splat(blk[i][:, R + j + t : R + j + t + 1]) for t in range(4)]
                up = (c[0] * q0 + c[1] * q1) + (c[2] * q2 + c[3] * q3)
                blk[i] = blk[i] - (jnp.where(sub >= 4, up, 0.0) if i == jb else up)
            if chol:
                g0 = lax.rsqrt(p00)
                l1 = p01 * g0
                w0 = r0 * g0
                g1 = lax.rsqrt(p11 - l1 * l1)
                w1 = (r1 - l1 * w0) * g1
                ratio = s23 / s22
                w2 = z2 * lax.rsqrt(s22)
                w3 = (z3 - ratio * z2) * lax.rsqrt(s33 - s23 * ratio)
                keep = (w0, w1, w2, w3)
            else:
                keep = (q0, q1, q2, q3)
            acc = out[jb] if js else jnp.zeros(wide, F32)
            for t in range(4):
                acc = jnp.where(sub == js + t, keep[t], acc)
            out[jb] = acc
    res = []
    for blk, out in zip(blocks, done):
        rows = jnp.concatenate(out, axis=0)[:, :R]
        res.append(rows if chol else dot3(jnp.concatenate(blk, axis=0)[:, :R], rows, TN))
    return res


def inverses(grams):
    diag = eye_mask()
    shifts = [shift_of(g, diag) for g in grams]
    mats = [jnp.where(diag, g * (1.0 / s) + 1.0, g * (1.0 / s)) for g, s in zip(grams, shifts)]
    return shifts, eliminate(mats)


def ident():
    return jnp.where(eye_mask(), 1.0, 0.0).astype(F32)


def place():
    core, z = lax.axis_index("rows") % 2, lax.axis_index("upd")
    g = z // 4
    o = 2 - (g + core) % 2
    return core, z, g, o, 2 * o - 3


def half_rows(ref, k, c):
    return ref[k, :, pl.ds(c, 1), :, :].reshape(512, 2 * R)


def panel_rows(ref, k):
    return ref[:, k, :, :].reshape(512, 2 * R)


def core_major(sk):
    lane = lax.broadcasted_iota(jnp.int32, (R, 128), 1)
    halves = [[], []]
    for m in range(4):
        a, b = sk[:, 256 * m : 256 * m + 128], sk[:, 256 * m + 128 : 256 * m + 256]
        a64, a96 = pltpu.roll(a, 64, 1), pltpu.roll(a, 96, 1)
        b32, b64 = pltpu.roll(b, 32, 1), pltpu.roll(b, 64, 1)
        for half, parts in zip(halves, ((a, a96, b64, b32), (a96, a64, b32, b))):
            low = jnp.where(lane < 32, parts[0], parts[1])
            high = jnp.where(lane < 96, parts[2], parts[3])
            half.append(jnp.where(lane < 64, low, high))
    return jnp.concatenate(halves[0] + halves[1], axis=1)


def leaf_pre(tile_ref, own_ref, sk_ref, part_ref, vt_ref, split_ref):
    core = place()[0]
    sh, sl = split(core_major(sk_ref[...]))
    split_ref[:R] = sh
    split_ref[R:] = sl
    r = lax.broadcasted_iota(jnp.int32, (R, 2 * R), 0)
    c = lax.broadcasted_iota(jnp.int32, (R, 2 * R), 1)
    pick = jnp.where(c == r + R, 1.0, 0.0).astype(BF16)
    so = split_ref[:, pl.ds(pl.multiple_of(core * 512, 512), 512)]
    for k in range(8):
        vt = mm(pick, half_rows(tile_ref, k, core), NT).astype(BF16)
        vt_ref[k] = mm(pick, half_rows(tile_ref, k, 1 - core), NT).astype(BF16)
        part_ref[k] = mm(jnp.concatenate([so, vt], axis=0), panel_rows(own_ref, k))


def leaf_y(w_ref, tile_ref, oth_ref, part_ref, vt_ref, split_ref, y_ref, inner_ref):
    core = place()[0]
    so = split_ref[:, pl.ds(pl.multiple_of((1 - core) * 512, 512), 512)]
    zero = jnp.zeros((R, R), F32)
    acc = None
    for p in range(4):
        dts = []
        for k in (2 * p, 2 * p + 1):
            res = part_ref[k] + mm(jnp.concatenate([so, vt_ref[k]], axis=0), panel_rows(oth_ref, k))
            proj = (res[:R] + res[R : 2 * R])[:, :R]
            inner = res[2 * R :][:, R:] * w_ref[k].astype(F32)
            inner_ref[k] = inner
            dts += [dot3(proj, inner, NT), zero]
        dh, dl = split(jnp.concatenate(dts, axis=1))
        tiles = jnp.concatenate([tile_ref[k].reshape(1024, 2 * R) for k in (2 * p, 2 * p + 1)], axis=1)
        out = mm(jnp.concatenate([dh, dl], axis=0), tiles, NT)
        out = out[:R] + out[R:]
        acc = out if acc is None else acc + out
    y_ref[...] = acc


def leaf_x(tile_ref, own_ref, oth_ref, y_ref, inner_ref, x_ref):
    core = place()[0]
    yh, yl = split(y_ref[...])
    ys = jnp.concatenate([yh, yl], axis=0)
    zero = jnp.zeros((R, R), F32)
    accs = [None, None]
    for p in range(4):
        ks = (2 * p, 2 * p + 1)
        ht = mm(ys, jnp.concatenate([tile_ref[k].reshape(1024, 2 * R) for k in ks], axis=1))
        ht = ht[:R] + ht[R:]
        ets = []
        for i, k in enumerate(ks):
            ets += [dot3(ht[:, 2 * R * i : 2 * R * i + R], inner_ref[k]), zero]
        eh, el = split(jnp.concatenate(ets, axis=1))
        es = jnp.concatenate([eh, el], axis=0)
        for h, ref in enumerate((own_ref, oth_ref)):
            out = mm(es, jnp.concatenate([panel_rows(ref, k) for k in ks], axis=1), NT)
            out = out[:R] + out[R:]
            accs[h] = out if accs[h] is None else accs[h] + out
    x_ref[:, pl.ds(pl.multiple_of(core * 512, 512), 512)] = accs[0]
    x_ref[:, pl.ds(pl.multiple_of((1 - core) * 512, 512), 512)] = accs[1]


def lanes(mats):
    return jnp.concatenate(mats, axis=1)


def rows_of(mats):
    return jnp.concatenate(mats, axis=0)


def put_shift(s):
    return jnp.broadcast_to(s, (8, 2 * R))


def group_y(y0, y1, y2, y3, out_ref, k_ref, j_ref, s_ref):
    stack = rows_of([y0[...], y1[...], y2[...], y3[...]])
    ah, al = split(stack)
    gram = mm(ah, ah, NT) + (mm(ah, al, NT) + mm(al, ah, NT))
    k_ref[...] = gram
    eye = ident()
    shifts, js = inverses([gram[R * u : R * u + R, R * u : R * u + R] for u in range(4)])
    rs = [eye - j for j in js]
    pair_r = [lanes(rs[0:2]), lanes(rs[2:4])]
    grams = []
    for m in range(2):
        kp = gram[2 * R * m : 2 * R * m + 2 * R, 2 * R * m : 2 * R * m + 2 * R]
        grams.append(dot3(dot3(pair_r[m], kp), rows_of(rs[2 * m : 2 * m + 2])))
    shifts2, js2 = inverses(grams)
    pt = lanes([dot3(eye - js2[m], pair_r[m]) for m in range(2)])
    ph, plo = split(pt)
    out_ref[...] = mm(ph, ah) + (mm(ph, al) + mm(plo, ah))
    for u, j in enumerate(js + js2):
        j_ref[u] = j
    for u, s in enumerate(shifts + shifts2):
        s_ref[u] = put_shift(1.0 / s)


def group_x(x0, x1, x2, x3, k_ref, j_ref, s_ref, send_ref, keep_ref):
    eye = ident()
    gram = k_ref[...]
    js = [j_ref[u] for u in range(6)]
    ss = [s_ref[u][:1, :1] for u in range(6)]
    rs = [eye - j for j in js]
    pt, q1 = [], []
    for m in range(2):
        pr = lanes(rs[2 * m : 2 * m + 2])
        kp = gram[2 * R * m : 2 * R * m + 2 * R, 2 * R * m : 2 * R * m + 2 * R]
        rk = dot3(pr, kp)
        q1.append(
            lanes([dot3(rk[:, :R] * ss[2 * m], js[2 * m]), dot3(rk[:, R:] * ss[2 * m + 1], js[2 * m + 1])])
        )
        pt.append(dot3(rs[4 + m], pr))
    pk = dot3(lanes(pt), gram)
    qt = []
    for m in range(2):
        t = dot3(pk[:, 2 * R * m : 2 * R * m + 2 * R], rows_of(rs[2 * m : 2 * m + 2]))
        t = dot3(t * ss[4 + m], js[4 + m])
        qt.append(dot3(t, q1[m]))
    qh, ql = split(lanes(qt))
    refs = (x0, x1, x2, x3)
    g = place()[2]
    sib = g + 1 - 2 * (g % 2)
    for dst, blocks in ((send_ref, (sib, 3 - sib)), (keep_ref, (g, 3 - g))):
        spots = [pl.ds(pl.multiple_of(512 * c + block * 128, 128), 128) for block in blocks for c in range(2)]
        xh, xl = split(rows_of([lanes([x[:, at] for at in spots]) for x in refs]))
        dst[...] = mm(qh, xh) + (mm(qh, xl) + mm(ql, xh))


def merge_y(y0, y1, out_ref, k_ref, j_ref, s_ref):
    ah, al = split(rows_of([y0[...], y1[...]]))
    gram = mm(ah, ah, NT) + (mm(ah, al, NT) + mm(al, ah, NT))
    k_ref[...] = gram
    eye = ident()
    shifts, js = inverses([gram[R * u : R * u + R, R * u : R * u + R] for u in range(2)])
    ph, plo = split(lanes([eye - j for j in js]))
    out_ref[...] = mm(ph, ah) + (mm(ph, al) + mm(plo, ah))
    for u in range(2):
        j_ref[u] = js[u]
        s_ref[u] = put_shift(1.0 / shifts[u])


def merge_q(gram, js, ss):
    eye = ident()
    rk = dot3(lanes([eye - j for j in js]), gram)
    return lanes([dot3(rk[:, R * u : R * u + R] * ss[u], js[u]) for u in range(2)])


def merge_x(x0, x1, k_ref, j_ref, s_ref, send_ref, keep_ref):
    qt = merge_q(k_ref[...], [j_ref[u] for u in range(2)], [s_ref[u][:1, :1] for u in range(2)])
    out = dot3(qt, rows_of([x0[...], x1[...]]))
    keep_ref[...] = out[:, :256]
    send_ref[...] = out[:, 256:]


def root_y(y0, y1, w_ref, f_ref):
    ah, al = split(rows_of([y0[...], y1[...]]))
    gram = mm(ah, ah, NT) + (mm(ah, al, NT) + mm(al, ah, NT))
    eye = ident()
    shifts, js = inverses([gram[R * u : R * u + R, R * u : R * u + R] for u in range(2)])
    rs = [eye - j for j in js]
    pr = lanes(rs)
    g = dot3(dot3(pr, gram), rows_of(rs))
    diag = eye_mask()
    s = shift_of(g, diag)
    rec = 1.0 / s
    (ci,) = eliminate([jnp.where(diag, g * rec + 1.0, g * rec)], chol=True)
    ci = ci * lax.rsqrt(s)
    f_ref[...] = dot3(ci, merge_q(gram, js, [1.0 / v for v in shifts]))
    at = pl.multiple_of(place()[2] * 256, 256)
    yr = rows_of([y0[:, pl.ds(at, 256)], y1[:, pl.ds(at, 256)]])
    w_ref[...] = dot3(dot3(ci, pr), yr) * 32.0


def root_out(w_ref, f_ref, x0, x1, o0, o1, o2, o3, buf):
    zt = dot3(f_ref[...], rows_of([x0[...], x1[...]])) * (1.0 / 32.0)
    both = rows_of([w_ref[...], zt]).T
    natural = rows_of([both[128 * c + 32 * j : 128 * c + 32 * j + 32] for j in range(4) for c in range(2)])
    lane = lax.broadcasted_iota(jnp.int32, (256, 2 * R), 1)
    buf[...] = jnp.where(lane < R, both, natural)
    _, z, g, o, e = place()
    mine = jnp.where(z == 4 * g + o, 1, 0)

    def block(j):
        return buf[pl.ds(pl.multiple_of(j * R, R), R), :]

    o0[...] = jnp.where(jnp.full((R, 2 * R), mine) == 1, block(o), 0.0)
    o1[...], o2[...], o3[...] = block(o + e), block(o - e), block(o - 2 * e)


def shape(*dims, dtype=F32):
    return jax.ShapeDtypeStruct(dims, dtype)


def call(fn, outs, n_smem, args, scratch=(), flops=10**8):
    specs = [SMEM] * n_smem + [VMEM] * (len(args) - n_smem)
    many = isinstance(outs, (tuple, list))
    kernel = pl.pallas_call(
        fn,
        out_shape=outs,
        in_specs=specs,
        out_specs=[VMEM] * len(outs) if many else VMEM,
        scratch_shapes=list(scratch),
        cost_estimate=pl.CostEstimate(flops=flops, bytes_accessed=10**6, transcendentals=0),
        compiler_params=pltpu.CompilerParams(vmem_limit_bytes=20 * 2**20),
    )
    return kernel(*args)


OWNERS = ((2, 5, 10, 13), (1, 6, 9, 14))
SIDE = ((1, -1, 1, -1), (-1, 1, -1, 1))


def over_rows(per_core, rows, upd):
    return [(r * upd + a, r * upd + b) for r in range(rows) for a, b in per_core[r % 2]]


def tables(rows, upd):
    member = []
    for off in (1, -1, -2):
        member.append([[(o + off * e, o) for o, e in zip(OWNERS[c], SIDE[c])] for c in range(2)])
    third = [[(OWNERS[c][i], OWNERS[c][i ^ 1]) for i in range(4)] for c in range(2)]
    fourth = [[(OWNERS[c][i], OWNERS[c][3 - i]) for i in range(4)] for c in range(2)]
    back = [[[(b, a) for a, b in m[c]] for c in range(2)] for m in member]
    full = lambda p: over_rows(p, rows, upd)
    return [full(m) for m in member], full(third), full(fourth), [full(m) for m in back]


def tree(y, leaf_x_of, rows, upd):
    members, third, fourth, back = tables(rows, upd)

    def send(v, perm):
        return lax.ppermute(v, ("rows", "upd"), perm)

    ys = [y] + [send(y, m) for m in members]
    x = leaf_x_of(y)
    xs = [x] + [send(x, m) for m in members]
    sizes = (shape(R, 1024), shape(256, 256), shape(6, R, R), shape(6, 8, 128))
    y2, k2, j2, s2 = call(group_y, sizes, 0, ys)
    y2h = send(y2, third)
    xsend, xkeep = call(group_x, (shape(R, 512), shape(R, 512)), 0, [*xs, k2, j2, s2])
    xh = send(xsend, third)
    sizes = (shape(R, 1024), shape(128, 128), shape(2, R, R), shape(2, 8, 128))
    y3, k3, j3, s3 = call(merge_y, sizes, 0, [y2, y2h])
    y3h = send(y3, fourth)
    xsend, xkeep = call(merge_x, (shape(R, 256), shape(R, 256)), 0, [xkeep, xh, k3, j3, s3])
    xh = send(xsend, fourth)
    wt, f = call(root_y, (shape(R, 256), shape(R, 128)), 0, [y3, y3h])
    buf = [pltpu.VMEM((256, 128), F32)]
    outs = call(root_out, [shape(R, 128)] * 4, 0, [wt, f, xkeep, xh], scratch=buf)
    res = outs[0]
    for o, p in zip(outs[1:], back):
        res = res + send(o, p)
    return res


def local_update(tiles, own, oth, nonnull, sketch, rows, upd):
    tiles = tiles.reshape(8, 16, 2, 32, 2 * R)
    pre = (shape(8, 3 * R, 2 * R), shape(8, R, 512, dtype=BF16), shape(2 * R, 1024, dtype=BF16))
    part, vt, halves = call(leaf_pre, pre, 0, [tiles, own, sketch])
    y, inner = call(
        leaf_y, (shape(R, 1024), shape(8, R, R)), 1, [nonnull, tiles, oth, part, vt, halves]
    )

    def leaf_x_of(y):
        return call(leaf_x, shape(R, 1024), 0, [tiles, own, oth, y, inner])

    return tree(y, leaf_x_of, rows, upd)


def body(tile_factors, panel_factors, nonnull, sketch):
    rows, upd = lax.axis_size("rows"), lax.axis_size("upd")
    same = [[2 * i + c for i in range(rows // 2)] for c in range(2)]
    blocks = jnp.broadcast_to(panel_factors[None], (rows // 2,) + panel_factors.shape)
    own = lax.all_to_all(blocks, "rows", 0, 0, axis_index_groups=same)
    oth = lax.ppermute(own, "rows", [(i, i ^ 1) for i in range(rows)])
    return local_update(tile_factors[0], own, oth, nonnull[0], sketch, rows, upd)[None]


def solution(mesh):
    in_specs = (P("rows", "upd", None, None), P("upd", "rows", None), P("rows", "upd"), P())
    out_specs = P("rows", "upd", None)
    return jax.shard_map(body, mesh=mesh, in_specs=in_specs, out_specs=out_specs, check_vma=False)
```
